512 devices in a mesh: shell: 128 (over x, z, core), aux: 4 (over y).
Axes of the slice: x: 4, y: 4, z: 16, core: 2. Of those that a mesh axis runs over, the one named last changes fastest.
Arguments:
- integrals: bfloat16 [512, 128, 4, 128], P('shell', None, 'aux'), may hold values from -6 to 6
- pair_list: int32 [512, 3], P('shell'), may hold values from 0 to 511, as said below
- coef: bfloat16 [65536, 1024], P('shell'), may hold values from -0.5 to 0.5
- metric: bfloat16 [4, 4], replicated, may hold values from -3 to 3, as said below
- occ_slot: int32 [128], replicated, may hold values from 0 to 127, each once
Outputs:
- transformed: bfloat16 [1024, 4, 65536], P(('shell', 'aux'))
The draws below stay inside these ranges and needn't reach their ends.
Inputs may be any that keep to these rules, and one draw needn't show every extreme that they name: `pair_list`: row d * 4 + k holds slot k of index d of shell: block row, block column, live flag. The block column lies in d * 4 to (d + 1) * 4 - 1. On every index live slots come first and at least one is live; some index has all 4 live. `metric`: lower triangular, positive on the diagonal.
All inputs are finite; a program needn't handle non-finite values.
Results may differ from the reference program's by a relative error of at most 0.0054.
Values may be sent and summed in bfloat16 or wider, within the bound.
A program may use at most 64 MiB of HBM per device.

```python
import jax
import jax.numpy as jnp
from jax import lax

BS = 128
NOCC = 1024
OB = 8
NB_DEV = 4
PAIRS_DEV = 4
NB = 512
NBF = 65536
SLAB = 4
PAIRS = 512
NOB = 128


def draw_pair_list(key, part):
    keys = jax.random.split(jax.random.fold_in(key, 11), 4)
    device_count = PAIRS // PAIRS_DEV
    positions = jnp.arange(PAIRS, dtype=jnp.int32)
    owner = positions // PAIRS_DEV
    within = positions % PAIRS_DEV
    block_rows = jax.random.randint(keys[0], (PAIRS,), 0, NB, dtype=jnp.int32)
    block_cols = owner * NB_DEV + jax.random.randint(keys[1], (PAIRS,), 0, NB_DEV, dtype=jnp.int32)
    counts = jax.random.randint(keys[2], (device_count,), 1, PAIRS_DEV + 1, dtype=jnp.int32)
    full_device = jax.random.randint(keys[3], (), 0, device_count, dtype=jnp.int32)
    counts = jnp.where(jnp.arange(device_count, dtype=jnp.int32) == full_device, PAIRS_DEV, counts)
    block_rows = jnp.where(positions == full_device * PAIRS_DEV, NB - 1, block_rows)
    live_flag = (within < counts[owner]).astype(jnp.int32)
    return jnp.stack([block_rows, block_cols, live_flag], axis=1).astype(jnp.int32)


def draw_metric(key, part):
    keys = jax.random.split(jax.random.fold_in(key, 7), 2)
    spread = 0.35 * jnp.clip(jax.random.normal(keys[0], (SLAB, SLAB), jnp.float32), -5.0, 5.0)
    diagonal = jax.random.uniform(keys[1], (SLAB,), jnp.float32, 0.7, 1.3)
    lower = jnp.tril(spread, -1) + jnp.diag(diagonal)
    return lower.astype(jnp.bfloat16)


def levels(key, dims, pieces, low, high):
    level, own = 1.0, jax.random.fold_in(key, 6)
    for axis_at, blocks in pieces:
        steps = jnp.exp(jax.random.uniform(jax.random.fold_in(own, axis_at), (blocks,), jnp.float32, low / len(pieces), high / len(pieces)))
        level = level * jnp.repeat(steps, dims[axis_at] // blocks).reshape([-1 if axis == axis_at else 1 for axis in range(len(dims))])
    return level


def centred(rng, extent, width, reach, cuts=(), kind=jnp.bfloat16):
    entries = width * jax.random.normal(rng, extent, jnp.float32)
    if cuts:
        entries = entries * levels(rng, extent, cuts, -0.22, 0.18)
    return jnp.clip(entries, -reach, reach).astype(kind)


def setup_inputs(seed: int = 0) -> dict:
    splits = jax.random.split(jax.random.key(seed), 6)
    return {
        "integrals": centred(splits[0], (PAIRS, BS, SLAB, BS), 1.0, 6.0, ((0, 128), (2, 4))),
        "pair_list": draw_pair_list(jax.random.fold_in(splits[5], 71), 0),
        "coef": centred(splits[2], (NBF, NOCC), BS ** -0.5, 0.5, ((0, 128),)),
        "metric": draw_metric(jax.random.fold_in(splits[5], 71), 0),
        "occ_slot": jax.random.permutation(splits[4], NOB).astype(jnp.int32),
    }


def reference(integrals, pair_list, coef, metric, occ_slot):
    inverse = jnp.zeros((NOB,), jnp.int32).at[occ_slot].set(jnp.arange(NOB, dtype=jnp.int32))
    ordered = jnp.take(coef.reshape(NBF, NOB, OB), inverse, axis=1).reshape(NBF, NOCC)

    def accumulate(running, item):
        int_block, pair_entry = item
        column = lax.dynamic_slice_in_dim(ordered, (pair_entry[1] * BS).astype(jnp.int32), BS, 0)
        product = jnp.dot(column.T, int_block.reshape(BS, SLAB * BS), preferred_element_type=jnp.float32)
        rounded = lax.optimization_barrier(product.astype(jnp.bfloat16)).astype(jnp.float32)
        rounded = rounded * pair_entry[2].astype(jnp.float32)
        offset = (pair_entry[0] * BS).astype(jnp.int32)
        anchor = jnp.zeros((), jnp.int32)
        current = lax.dynamic_slice(running, (anchor, anchor, offset), (NOCC, SLAB, BS))
        running = lax.dynamic_update_slice(running, current + rounded.reshape(NOCC, SLAB, BS), (anchor, anchor, offset))
        return running, None

    initial = jnp.zeros((NOCC, SLAB, NBF), jnp.float32)
    summed, unused = lax.scan(accumulate, initial, (integrals, pair_list))
    summed = lax.optimization_barrier(summed.astype(jnp.bfloat16))
    factor = metric.astype(jnp.float32)

    def transform_rows(rows):
        return jnp.einsum("qp,ipm->iqm", factor, rows.astype(jnp.float32)).astype(jnp.bfloat16)

    result = lax.map(transform_rows, summed.reshape(NOB, OB, SLAB, NBF))
    return result.reshape(NOCC, SLAB, NBF)
```

```python
import jax
import jax.numpy as jnp
from jax import lax
from jax.experimental import pallas as pl
from jax.experimental.pallas import tpu as pltpu
from jax.sharding import PartitionSpec as P

MESH = pl.DeviceIdType.MESH
BS = 128
OB = 8
NX, NZ, NC, NY = 4, 16, 2, 4
NQ = NX * NC
SLOTS = 4
BLK = SLOTS * BS
ROWS = BLK + 16
CH = 3
CR = ROWS // CH
GROUPS = 9
F32, BF, I32 = jnp.float32, jnp.bfloat16, jnp.int32


def dev(x, z, c, y):
    return ((x * NZ + z) * NC + c, y)


def span(g):
    if g == 0:
        return 0, 1
    if g == 8:
        return 15, 1
    return 2 * g - 1, 2


def move_kernel(
    pair_ref, occ_ref, int_ref, coef_ref, out_ref, rows_ref,
    coef, blk, made, ct, half, relay, tab, tabs,
    s_loc, s_own, ring_s, ring_r, cz_s, cz_r, cy_s, cy_r, x_s, x_r, y_s, y_r, t_s, t_r, xl, yl,
):
    s = lax.axis_index("shell")
    y = lax.axis_index("aux")
    x, z, c = s // (NZ * NC), (s // NC) % NZ, s % NC
    q = x * NC + c
    sg = 1 - 2 * c

    load_coef = pltpu.make_async_copy(coef_ref, coef, s_loc)
    load_coef.start()
    load_int = pltpu.make_async_copy(int_ref, blk.at[0, pl.ds(0, BLK)], s_own)
    load_int.start()

    barrier = pltpu.get_barrier_semaphore()
    peers = [dev(x, (z + d) % NZ, cc, y) for d in range(1, NZ) for cc in range(NC)]
    peers.append(dev(x, z, 1 - c, y))
    peers += [dev((x + d) % NX, z, cc, y) for d in range(1, NX) for cc in range(NC)]
    peers += [dev(x, z, c, (y + d) % NY) for d in range(1, NY)]
    for p in peers:
        pl.semaphore_signal(barrier, inc=1, device_id=p, device_id_type=MESH)

    rid = lax.broadcasted_iota(I32, (16, BS), 0)
    k16 = (rid // 2) % SLOTS
    rv = jnp.zeros((16, BS), I32)
    for k in range(SLOTS):
        rv = jnp.where(k16 == k, pair_ref[k, 0], rv)
    rv = jnp.where(rid < 8, rv // 16, rv % 16)
    blk[0, pl.ds(BLK, 16)] = rv.astype(F32).astype(BF)
    load_int.wait()
    pl.semaphore_wait(barrier, len(peers))

    pending = []

    def remote(src, dst, ss, rs, to):
        m = pltpu.make_async_remote_copy(
            src_ref=src, dst_ref=dst, send_sem=ss, recv_sem=rs, device_id=to, device_id_type=MESH
        )
        m.start()
        pending.append(m)
        return m

    nxt = dev(x, (z + sg + NZ) % NZ, c, y)
    landed = {}

    def ring(j_from, j_to, ch, to):
        part = pl.ds(ch * CR, CR)
        landed[(j_to, ch)] = remote(
            blk.at[j_from, part], blk.at[j_to, part], ring_s.at[j_to, ch], ring_r.at[j_to, ch], to
        )

    for ch in range(CH):
        ring(0, 1, ch, nxt)
        ring(0, 16, ch, dev(x, z, 1 - c, y))

    lane_b = lax.broadcasted_iota(I32, (BS, NZ * NQ * OB), 0)
    col_b = lax.broadcasted_iota(I32, (BS, NZ * NQ * OB), 1)
    expand = jnp.where(col_b // OB == lane_b, 1.0, 0.0).astype(BF)
    occ8 = jnp.broadcast_to(occ_ref[...].astype(F32), (8, BS)).astype(BF)
    occ_col = jnp.dot(occ8, expand, preferred_element_type=F32)[0:1].astype(I32) * OB
    occ_col = occ_col + lax.broadcasted_iota(I32, (1, NZ * NQ * OB), 1) % OB
    load_coef.wait()
    all_coef = coef[...]
    cz = {}

    def forward_ring(d):
        for e in range(2):
            j = 16 if (d == 0 and e == 1) else 2 * d - 1 + e
            if j > 15 and d > 0:
                continue
            for ch in range(CH):
                landed[(j, ch)].wait_recv()
                if d < 7 or (d == 7 and e == 0):
                    ring(j, 2 * d + 1 + e, ch, nxt)

    for uc in range(4):
        rid = lax.broadcasted_iota(I32, (256, BS), 0) + uc * 256
        u, qq, k, o = rid // 64, (rid // 8) % NQ, (rid // 2) % SLOTS, rid % 2
        dist, other = (u + 1) // 2, (u + 1) % 2
        zz = (z + sg * (1 - 2 * other) * dist + NZ) % NZ
        want = (((qq // NC) * NZ + zz) * NC + qq % NC) * OB + y * 2 + o
        pick = jnp.concatenate(
            [
                jnp.where(want == occ_col[:, b * BS : (b + 1) * BS], 1.0, 0.0)
                for b in range(NZ * NQ * OB // BS)
            ],
            axis=1,
        ).astype(BF)
        got = lax.dot_general(pick, all_coef, (((1,), (1,)), ((), ())), preferred_element_type=F32)
        cv = jnp.full((256, BS), -1, I32)
        for kk in range(SLOTS):
            local = jnp.where(pair_ref[kk, 2] == 1, pair_ref[kk, 1] % SLOTS, -1)
            cv = jnp.where(k == kk, local, cv)
        chosen = jnp.zeros((256, BS), F32)
        for b in range(SLOTS):
            chosen = jnp.where(cv == b, got[:, b * BS : (b + 1) * BS], chosen)
        made[pl.ds(4 * uc, 4)] = chosen.astype(BF).reshape(4, 64, BS)
        if uc == 0:
            ct[0, y] = chosen[0:64].astype(BF)
        for uu in range(max(4 * uc, 1), 4 * uc + 4):
            d, e = (uu + 1) // 2, (uu + 1) % 2
            zt = (z + sg * (1 - 2 * e) * d + NZ) % NZ
            ctarget = c if e == 0 else 1 - c
            cz[uu] = remote(
                made.at[uu], ct.at[uu, y], cz_s.at[uu], cz_r.at[uu], dev(x, zt, ctarget, y)
            )
        if uc == 0:
            forward_ring_other(landed, ring, nxt)

    kmask = []
    kid = (lax.broadcasted_iota(I32, (256, BS), 0) // 2) % SLOTS
    for k in range(SLOTS):
        kmask.append(jnp.where(kid == k, 1.0, 0.0).astype(BF))

    cy, xs, ys, xloc, yloc = {}, {}, {}, {}, {}

    def coef_aux(g):
        j0, n = span(g)
        for j in range(j0, j0 + n):
            if j > 0:
                cz[j].wait_recv()
        for dy in range(1, NY):
            part = ct.at[pl.ds(j0, n), y]
            cy[(g, dy)] = remote(
                part, part, cy_s.at[g, dy], cy_r.at[g, dy], dev(x, z, c, (y + dy) % NY)
            )

    def compute(g):
        j0, n = span(g)
        for dy in range(1, NY):
            cy[(g, dy)].wait_recv()
        for j in range(j0, j0 + n):
            lhs = ct[j].reshape(256, BS)
            lhs = jnp.concatenate([lhs * kmask[k] for k in range(SLOTS)], axis=1)
            h = jnp.dot(lhs, blk[j, pl.ds(0, BLK)], preferred_element_type=F32)
            h = h.reshape(NY, NQ, 8, BS)
            for qq in range(NQ):
                half[j, qq] = h[:, qq].astype(BF)
        own = pltpu.make_async_copy(
            half.at[pl.ds(j0, n), q], relay.at[pl.ds(j0, n), :, q], xl.at[g]
        )
        own.start()
        xloc[g] = own
        for dq in range(1, NQ):
            qt = (q + dq) % NQ
            xs[(g, dq)] = remote(
                half.at[pl.ds(j0, n), qt], relay.at[pl.ds(j0, n), :, q],
                x_s.at[g, dq], x_r.at[g, dq], dev(qt // NC, z, qt % NC, y),
            )

    def to_aux(g):
        j0, n = span(g)
        xloc[g].wait()
        for dq in range(1, NQ):
            xs[(g, dq)].wait_recv()
        own = pltpu.make_async_copy(
            relay.at[pl.ds(j0, n), y], out_ref.at[y, pl.ds(j0, n)], yl.at[g]
        )
        own.start()
        yloc[g] = own
        for dy in range(1, NY):
            yt = (y + dy) % NY
            ys[(g, dy)] = remote(
                relay.at[pl.ds(j0, n), yt], out_ref.at[y, pl.ds(j0, n)],
                y_s.at[g, dy], y_r.at[g, dy], dev(x, z, c, yt),
            )

    coef_aux(0)
    coef_aux(1)
    for d in range(1, 9):
        forward_ring(d)
        if d + 1 < GROUPS:
            coef_aux(d + 1)
        compute(d - 1)
        if d >= 3:
            to_aux(d - 3)
    lane = lax.broadcasted_iota(I32, (8, BS), 1)
    table = jnp.zeros((8, BS), F32)
    for j in range(16):
        hi = blk[j, pl.ds(BLK, 16)].astype(F32)
        table = jnp.where(lane == j, hi[0:8] * 16.0 + hi[8:16], table)
    tab[...] = table
    tabs[q] = table
    ts = []
    for dq in range(1, NQ):
        qt = (q + dq) % NQ
        ts.append(
            remote(tab, tabs.at[q], t_s.at[dq], t_r.at[dq], dev(qt // NC, z, qt % NC, y))
        )
    compute(8)
    for g in (6, 7, 8):
        to_aux(g)
    for m in ts:
        m.wait_recv()
    rows_ref[...] = tabs[...]
    for g in range(GROUPS):
        yloc[g].wait()
        for dy in range(1, NY):
            ys[(g, dy)].wait_recv()
    for m in pending:
        m.wait_send()


def forward_ring_other(landed, ring, nxt):
    for ch in range(CH):
        landed[(16, ch)].wait_recv()
        ring(16, 2, ch, nxt)


def sum_kernel(metric_ref, rows_ref, part_ref, out_ref):
    nrho = 1024
    rho = lax.broadcasted_iota(I32, (BS, nrho), 1)
    lane = lax.broadcasted_iota(I32, (BS, nrho), 0)
    by_block = jnp.where(rho // 64 == lane, 1.0, 0.0).astype(BF)
    table = rows_ref[...].reshape(64, BS)
    hi = jnp.floor(table * (1.0 / 16.0))
    lo = table - hi * 16.0
    spread = 16.0 * jnp.dot(hi.astype(BF), by_block, preferred_element_type=F32)
    spread = spread + jnp.dot(lo.astype(BF), by_block, preferred_element_type=F32)
    r64 = lax.broadcasted_iota(I32, (64, nrho), 0)
    c64 = lax.broadcasted_iota(I32, (64, nrho), 1)
    block_row = jnp.sum(jnp.where(c64 % 64 == r64, spread, 0.0), axis=0, keepdims=True)
    o_row = lax.broadcasted_iota(I32, (1, nrho), 1) % 2
    code = block_row.astype(I32) + o_row * 512

    gi = lax.broadcasted_iota(I32, (256, 256), 0)
    gj = lax.broadcasted_iota(I32, (256, 256), 1)
    same = gi // 4 == gj % 64
    mix = jnp.zeros((256, 256), F32)
    for a in range(NY):
        for b in range(NY):
            mix = jnp.where(same & (gi % 4 == a) & (gj // 64 == b), metric_ref[a, b], mix)
    mix = mix.astype(BF)

    parts = jnp.concatenate([part_ref[p].reshape(nrho, BS) for p in range(NY)], axis=1)
    for t in range(4):
        row = lax.broadcasted_iota(I32, (256, nrho), 0) + t * 256
        match = jnp.where(row == code, 1.0, 0.0).astype(BF)
        total = jnp.dot(match, parts, preferred_element_type=F32).astype(BF)
        for b in range(4):
            stack = jnp.concatenate(
                [total[b * 64 : (b + 1) * 64, p * BS : (p + 1) * BS] for p in range(NY)], axis=0
            )
            mixed = jnp.dot(mix, stack, preferred_element_type=F32)
            out_ref[pl.ds((t * 4 + b) * 256, 256)] = mixed.astype(BF)


def per_device(integrals, pair_list, coef, metric, occ_slot):
    dma = pltpu.SemaphoreType.DMA
    any_ = pl.BlockSpec(memory_space=pl.ANY)
    vmem = pl.BlockSpec(memory_space=pltpu.VMEM)
    smem = pl.BlockSpec(memory_space=pltpu.SMEM)
    parts, rows = pl.pallas_call(
        move_kernel,
        name="move",
        out_shape=(
            jax.ShapeDtypeStruct((NY, NZ, NQ, 8, BS), BF),
            jax.ShapeDtypeStruct((NQ, 8, BS), F32),
        ),
        in_specs=[smem, vmem, any_, any_],
        out_specs=(any_, vmem),
        scratch_shapes=[
            pltpu.VMEM((4 * BS, 1024), BF),
            pltpu.VMEM((17, ROWS, BS), BF),
            pltpu.VMEM((NZ, 64, BS), BF),
            pltpu.VMEM((NZ, NY, 64, BS), BF),
            pltpu.VMEM((NZ, NQ, NY, 8, BS), BF),
            pltpu.VMEM((NZ, NY, NQ, 8, BS), BF),
            pltpu.VMEM((8, BS), F32),
            pltpu.VMEM((NQ, 8, BS), F32),
            dma,
            dma,
            dma((17, CH)),
            dma((17, CH)),
            dma((NZ,)),
            dma((NZ,)),
            dma((GROUPS, NY)),
            dma((GROUPS, NY)),
            dma((GROUPS, NQ)),
            dma((GROUPS, NQ)),
            dma((GROUPS, NY)),
            dma((GROUPS, NY)),
            dma((NQ,)),
            dma((NQ,)),
            dma((GROUPS,)),
            dma((GROUPS,)),
        ],
        compiler_params=pltpu.CompilerParams(
            collective_id=0, has_side_effects=True, vmem_limit_bytes=40 << 20
        ),
    )(pair_list, occ_slot.reshape(1, BS), integrals.reshape(BLK, BS), coef)
    out = pl.pallas_call(
        sum_kernel,
        name="sums",
        out_shape=jax.ShapeDtypeStruct((4096, BS), BF),
        in_specs=[smem, vmem, vmem],
        out_specs=vmem,
        compiler_params=pltpu.CompilerParams(vmem_limit_bytes=40 << 20),
    )(metric.astype(F32), rows, parts)
    return out.reshape(2, 512, NY, BS).transpose(0, 2, 1, 3).reshape(2, NY, 512 * BS)


def solution(mesh):
    placed = (P("shell", None, "aux", None), P("shell", None), P("shell", None), P(), P())
    return jax.shard_map(
        per_device,
        mesh=mesh,
        in_specs=placed,
        out_specs=P(("shell", "aux"), None, None),
        check_vma=False,
    )
```

```python
import jax
import jax.numpy as jnp
from jax import lax
from jax.experimental import pallas as pl
from jax.experimental.pallas import tpu as pltpu
from jax.sharding import PartitionSpec as P

MESH = pl.DeviceIdType.MESH
BS = 128
OB = 8
NX, NZ, NC, NY = 4, 16, 2, 4
NQ = NX * NC
SLOTS = 4
BLK = SLOTS * BS
ROWS = BLK + 16
CUTS = ((0, 256), (256, ROWS - 256))
SPANS = ((0, 3), (3, 2), (5, 2), (7, 2), (9, 2), (11, 2), (13, 2), (15, 1))
GROUPS = len(SPANS)
F32, BF, I32 = jnp.float32, jnp.bfloat16, jnp.int32


def dev(x, z, c, y):
    return ((x * NZ + z) * NC + c, y)


def move_kernel(
    pair_hbm, occ_hbm, int_ref, coef_ref, sums_ref,
    pair_ref, occ_ref, coef, blk, made, ct, half, relay, parts, total, tab, tabs,
    loc, ring_s, ring_r, cz_s, cz_r, cy_s, cy_r, x_s, x_r, y_s, y_r, t_s, t_r, xl, yl, met,
):
    s = lax.axis_index("shell")
    y = lax.axis_index("aux")
    x, z, c = s // (NZ * NC), (s // NC) % NZ, s % NC
    q = x * NC + c
    sg = 1 - 2 * c

    loads = [
        pltpu.make_async_copy(pair_hbm, pair_ref, loc.at[0]),
        pltpu.make_async_copy(int_ref, blk.at[0, pl.ds(0, BLK)], loc.at[1]),
        pltpu.make_async_copy(occ_hbm, occ_ref, loc.at[2]),
        pltpu.make_async_copy(coef_ref, coef, loc.at[3]),
    ]
    for m in loads:
        m.start()

    barrier = pltpu.get_barrier_semaphore()
    near = [dev(x, (z + 1) % NZ, c, y), dev(x, (z + NZ - 1) % NZ, c, y), dev(x, z, 1 - c, y)]
    peers = list(near)
    peers += [dev((x + d) % NX, z, cc, y) for d in range(1, NX) for cc in range(NC)]
    peers += [dev(x, z, c, (y + d) % NY) for d in range(1, NY)]
    for p in peers:
        pl.semaphore_signal(barrier, inc=1, device_id=p, device_id_type=MESH)

    loads[0].wait()
    rid = lax.broadcasted_iota(I32, (16, BS), 0)
    k16 = (rid // 2) % SLOTS
    rv = jnp.zeros((16, BS), I32)
    for k in range(SLOTS):
        rv = jnp.where(k16 == k, pair_ref[k, 0], rv)
    rv = jnp.where(rid < 8, rv // 16, rv % 16)
    blk[0, pl.ds(BLK, 16)] = rv.astype(F32).astype(BF)
    loads[1].wait()
    pl.semaphore_wait(barrier, len(peers))

    def greet(i, to):
        for p in to:
            pl.semaphore_signal(met.at[i], inc=1, device_id=p, device_id_type=MESH)

    def meet(i, n):
        pl.semaphore_wait(met.at[i], n)

    def apart(d):
        return [dev(x, (z + d) % NZ, c, y), dev(x, (z + NZ - d) % NZ, c, y)]

    pending = []

    def remote(src, dst, ss, rs, to):
        m = pltpu.make_async_remote_copy(
            src_ref=src, dst_ref=dst, send_sem=ss, recv_sem=rs, device_id=to, device_id_type=MESH
        )
        m.start()
        pending.append(m)
        return m

    def drain(keep):
        while len(pending) > keep:
            pending.pop(0).wait_send()

    nxt = dev(x, (z + sg + NZ) % NZ, c, y)
    landed = {}

    def ring(j_from, j_to, to):
        for ch, (r0, n) in enumerate(CUTS):
            if (j_from, ch) in landed:
                landed[(j_from, ch)].wait_recv()
            part = pl.ds(r0, n)
            landed[(j_to, ch)] = remote(
                blk.at[j_from, part], blk.at[j_to, part], ring_s.at[j_to, ch], ring_r.at[j_to, ch], to
            )

    def arrive(j):
        for ch in range(len(CUTS)):
            landed[(j, ch)].wait_recv()

    def step(d, e):
        j = 2 * d - 1 + e
        if d < 7 or (d == 7 and e == 0):
            ring(j, j + 2, nxt)
        else:
            arrive(j)

    ring(0, 1, nxt)
    ring(0, 16, dev(x, z, 1 - c, y))
    greet(0, near)

    ncol = NZ * NQ * OB
    loads[2].wait()
    lane_b = lax.broadcasted_iota(I32, (BS, ncol), 0)
    col_b = lax.broadcasted_iota(I32, (BS, ncol), 1)
    expand = jnp.where(col_b // OB == lane_b, 1.0, 0.0).astype(BF)
    occ8 = jnp.broadcast_to(occ_ref[...].astype(F32), (8, BS)).astype(BF)
    occ_col = jnp.dot(occ8, expand, preferred_element_type=F32)[0:1].astype(I32) * OB
    occ_col = occ_col + lax.broadcasted_iota(I32, (1, ncol), 1) % OB
    loads[3].wait()
    cz = {}

    def coef_chunk(uc):
        rid = lax.broadcasted_iota(I32, (256, BS), 0) + uc * 256
        u, qq, k, o = rid // 64, (rid // 8) % NQ, (rid // 2) % SLOTS, rid % 2
        dist, other = (u + 1) // 2, (u + 1) % 2
        zz = (z + sg * (1 - 2 * other) * dist + NZ) % NZ
        want = (((qq // NC) * NZ + zz) * NC + qq % NC) * OB + y * 2 + o
        pick = jnp.concatenate(
            [
                jnp.where(want == occ_col[:, b * BS : (b + 1) * BS], 1.0, 0.0)
                for b in range(ncol // BS)
            ],
            axis=1,
        ).astype(BF)
        got = lax.dot_general(
            pick, coef[...], (((1,), (1,)), ((), ())), preferred_element_type=F32
        )
        cv = jnp.full((256, BS), -1, I32)
        for kk in range(SLOTS):
            local = jnp.where(pair_ref[kk, 2] == 1, pair_ref[kk, 1] % SLOTS, -1)
            cv = jnp.where(k == kk, local, cv)
        chosen = jnp.zeros((256, BS), F32)
        for b in range(SLOTS):
            chosen = jnp.where(cv == b, got[:, b * BS : (b + 1) * BS], chosen)
        made[pl.ds(4 * uc, 4)] = chosen.astype(BF).reshape(4, 64, BS)
        if uc == 0:
            ct[0, y] = chosen[0:64].astype(BF)

    def coef_out(*dist):
        for d in dist:
            for e in range(2 if d < 8 else 1):
                u = 2 * d - 1 + e
                zt = (z + sg * (1 - 2 * e) * d + NZ) % NZ
                ctarget = c if e == 0 else 1 - c
                cz[u] = remote(
                    made.at[u], ct.at[u, y], cz_s.at[u], cz_r.at[u], dev(x, zt, ctarget, y)
                )

    coef_chunk(0)
    meet(0, 3)
    greet(1, apart(2))
    ring(16, 2, nxt)
    coef_out(1)
    coef_chunk(1)
    meet(1, 2)
    greet(2, apart(4))
    coef_out(2, 3)
    coef_chunk(2)
    step(1, 0)
    meet(2, 2)
    coef_out(4, 5)
    coef_chunk(3)
    step(1, 1)
    coef_out(6, 7, 8)

    kid = (lax.broadcasted_iota(I32, (256, BS), 0) // 2) % SLOTS
    kmask = [jnp.where(kid == k, 1.0, 0.0).astype(BF) for k in range(SLOTS)]
    cy, xs, ys, xloc, yloc = {}, {}, {}, {}, {}

    def coef_aux(g):
        j0, n = SPANS[g]
        for j in range(j0, j0 + n):
            if j > 0:
                cz[j].wait_recv()
        for dy in range(1, NY):
            part = ct.at[pl.ds(j0, n), y]
            cy[(g, dy)] = remote(
                part, part, cy_s.at[g, dy], cy_r.at[g, dy], dev(x, z, c, (y + dy) % NY)
            )

    def compute(g):
        j0, n = SPANS[g]
        for dy in range(1, NY):
            cy[(g, dy)].wait_recv()
        for j in range(j0, j0 + n):
            lhs = ct[j].reshape(256, BS)
            lhs = jnp.concatenate([lhs * kmask[k] for k in range(SLOTS)], axis=1)
            h = jnp.dot(lhs, blk[j, pl.ds(0, BLK)], preferred_element_type=F32)
            h = h.reshape(NY, NQ, 8, BS)
            for qq in range(NQ):
                half[j, qq] = h[:, qq].astype(BF)
        here = pl.ds(j0, n)
        xloc[g] = pltpu.make_async_copy(half.at[here, q], relay.at[here, :, q], xl.at[g])
        xloc[g].start()
        for dq in range(1, NQ):
            qt = (q + dq) % NQ
            xs[(g, dq)] = remote(
                half.at[here, qt], relay.at[here, :, q],
                x_s.at[g, dq], x_r.at[g, dq], dev(qt // NC, z, qt % NC, y),
            )

    def to_aux(g):
        j0, n = SPANS[g]
        here = pl.ds(j0, n)
        xloc[g].wait()
        for dq in range(1, NQ):
            xs[(g, dq)].wait_recv()
        yloc[g] = pltpu.make_async_copy(relay.at[here, y], parts.at[y, here], yl.at[g])
        yloc[g].start()
        for dy in range(1, NY):
            yt = (y + dy) % NY
            ys[(g, dy)] = remote(
                relay.at[here, yt], parts.at[y, here],
                y_s.at[g, dy], y_r.at[g, dy], dev(x, z, c, yt),
            )

    def arrived(g):
        yloc[g].wait()
        for dy in range(1, NY):
            ys[(g, dy)].wait_recv()

    lane8 = lax.broadcasted_iota(I32, (8, BS), 1)
    tabled = {}

    def rows_out(i, j0, n):
        table = jnp.zeros((8, BS), F32)
        for j in range(j0, j0 + n):
            ids = blk[j, pl.ds(BLK, 16)].astype(F32)
            table = jnp.where(lane8 == j, ids[0:8] * 16.0 + ids[8:16], table)
        tab[i] = table
        tabs[i, q] = table
        for dq in range(1, NQ):
            qt = (q + dq) % NQ
            tabled[(i, dq)] = remote(
                tab.at[i], tabs.at[i, q], t_s.at[i, dq], t_r.at[i, dq], dev(qt // NC, z, qt % NC, y)
            )

    lane1 = lax.broadcasted_iota(I32, (1, BS), 1)
    code_of = {}

    def codes(i, j0, n):
        for dq in range(1, NQ):
            tabled[(i, dq)].wait_recv()
        turned = jnp.transpose(jnp.concatenate([tabs[i].reshape(64, BS)] * 2, axis=0))
        for j in range(j0, j0 + n, 2):
            both = jnp.where(lane1 < 64, turned[j : j + 1], turned[j + 1 : j + 2])
            code_of[j] = both.astype(I32) + (lane1 % 2) * 512

    def add_up(j0, n, first, last):
        code = [code_of[j] for j in range(j0, j0 + n, 2)]
        terms = jnp.concatenate(
            [parts[p, pl.ds(j0, n)].reshape(n * 64, BS) for p in range(NY)], axis=1
        )
        for t in range(4):
            row = lax.broadcasted_iota(I32, (256, BS), 0) + t * 256
            match = jnp.concatenate([jnp.where(row == v, 1.0, 0.0) for v in code], axis=1)
            got = jnp.dot(match.astype(BF), terms, preferred_element_type=F32)
            here = pl.ds(t * 256, 256)
            if first:
                total[here] = got
            elif last:
                sums_ref[here] = (total[here] + got).astype(BF)
            else:
                total[here] = total[here] + got

    coef_aux(0)
    step(2, 0)
    step(2, 1)
    coef_aux(1)
    compute(0)
    step(3, 0)
    step(3, 1)
    coef_aux(2)
    compute(1)
    to_aux(0)
    drain(24)
    step(4, 0)
    step(4, 1)
    coef_aux(3)
    compute(2)
    to_aux(1)
    drain(24)
    step(5, 0)
    step(5, 1)
    coef_aux(4)
    compute(3)
    to_aux(2)
    arrived(0)
    step(6, 0)
    step(6, 1)
    coef_aux(5)
    coef_aux(6)
    coef_aux(7)
    compute(4)
    rows_out(0, 0, 12)
    to_aux(3)
    step(7, 0)
    step(7, 1)
    compute(5)
    compute(6)
    to_aux(4)
    step(8, 0)
    compute(7)
    rows_out(1, 12, 4)
    to_aux(5)
    arrived(1)
    arrived(2)
    codes(0, 0, 12)
    add_up(0, 6, True, False)
    to_aux(6)
    to_aux(7)
    arrived(3)
    arrived(4)
    arrived(5)
    add_up(6, 6, False, False)
    codes(1, 12, 4)
    drain(6)
    arrived(6)
    arrived(7)
    add_up(12, 4, False, True)
    drain(0)


def mix_kernel(metric_ref, sums_ref, out_ref, mixed, sems):
    ri = lax.broadcasted_iota(I32, (256, 8), 0)
    ci = lax.broadcasted_iota(I32, (256, 8), 1)
    rows4 = jnp.where(ri % 4 == ci, 1.0, 0.0)[:, 0:4].astype(BF)
    rj = lax.broadcasted_iota(I32, (8, 256), 0)
    cj = lax.broadcasted_iota(I32, (8, 256), 1)
    cols4 = jnp.where(cj // 64 == rj, 1.0, 0.0)[0:4].astype(BF)
    spread = jnp.dot(rows4, metric_ref[...], preferred_element_type=F32).astype(BF)
    spread = jnp.dot(spread, cols4, preferred_element_type=F32)
    gi = lax.broadcasted_iota(I32, (256, 256), 0)
    gj = lax.broadcasted_iota(I32, (256, 256), 1)
    mix = jnp.where(gi // 4 == gj % 64, spread, 0.0).astype(BF)
    copies = []
    for t in range(4):
        for b in range(4 * t, 4 * t + 4):
            stack = jnp.concatenate(
                [sums_ref[pl.ds(b * 64, 64), p * BS : (p + 1) * BS] for p in range(NY)], axis=0
            )
            mixed[pl.ds(b * 256, 256)] = jnp.dot(mix, stack, preferred_element_type=F32).astype(BF)
        here = pl.ds(t * 1024, 1024)
        copies.append(pltpu.make_async_copy(mixed.at[here], out_ref.at[here], sems.at[t]))
        copies[-1].start()
    for m in copies:
        m.wait()


def per_device(integrals, pair_list, coef, metric, occ_slot):
    dma = pltpu.SemaphoreType.DMA
    hbm = pl.BlockSpec(memory_space=pltpu.HBM)
    vmem = pl.BlockSpec(memory_space=pltpu.VMEM)
    operands = (pair_list, occ_slot.reshape(1, BS), integrals.reshape(BLK, BS), coef)
    sums = pl.pallas_call(
        move_kernel,
        name="move",
        out_shape=jax.ShapeDtypeStruct((1024, NY * BS), BF),
        in_specs=[hbm, hbm, hbm, hbm],
        out_specs=vmem,
        scratch_shapes=[
            pltpu.SMEM((SLOTS, 3), I32),
            pltpu.VMEM((1, BS), I32),
            pltpu.VMEM((4 * BS, 1024), BF),
            pltpu.VMEM((17, ROWS, BS), BF),
            pltpu.VMEM((NZ, 64, BS), BF),
            pltpu.VMEM((NZ, NY, 64, BS), BF),
            pltpu.VMEM((NZ, NQ, NY, 8, BS), BF),
            pltpu.VMEM((NZ, NY, NQ, 8, BS), BF),
            pltpu.VMEM((NY, NZ, NQ, 8, BS), BF),
            pltpu.VMEM((1024, NY * BS), F32),
            pltpu.VMEM((2, 8, BS), F32),
            pltpu.VMEM((2, NQ, 8, BS), F32),
            dma((4,)),
            dma((17, len(CUTS))),
            dma((17, len(CUTS))),
            dma((NZ,)),
            dma((NZ,)),
            dma((GROUPS, NY)),
            dma((GROUPS, NY)),
            dma((GROUPS, NQ)),
            dma((GROUPS, NQ)),
            dma((GROUPS, NY)),
            dma((GROUPS, NY)),
            dma((2, NQ)),
            dma((2, NQ)),
            dma((GROUPS,)),
            dma((GROUPS,)),
            pltpu.SemaphoreType.REGULAR((3,)),
        ],
        compiler_params=pltpu.CompilerParams(
            collective_id=0, has_side_effects=True, vmem_limit_bytes=40 << 20
        ),
    )(*(pltpu.with_memory_space_constraint(a, pltpu.HBM) for a in operands))
    out = pl.pallas_call(
        mix_kernel,
        name="mix",
        out_shape=jax.ShapeDtypeStruct((4096, BS), BF),
        in_specs=[vmem, vmem],
        out_specs=hbm,
        scratch_shapes=[pltpu.VMEM((4096, BS), BF), dma((4,))],
        compiler_params=pltpu.CompilerParams(vmem_limit_bytes=40 << 20),
    )(metric, sums)
    return out.reshape(2, 512, NY, BS).transpose(0, 2, 1, 3).reshape(2, NY, 512 * BS)


def solution(mesh):
    placed = (P("shell", None, "aux", None), P("shell", None), P("shell", None), P(), P())
    return jax.shard_map(
        per_device,
        mesh=mesh,
        in_specs=placed,
        out_specs=P(("shell", "aux"), None, None),
        check_vma=False,
    )
```

```python
import jax
import jax.numpy as jnp
from jax import lax
from jax.experimental import pallas as pl
from jax.experimental.pallas import tpu as pltpu
from jax.sharding import PartitionSpec as P

MESH = pl.DeviceIdType.MESH
BS = 128
OB = 8
NX, NZ, NC, NY = 4, 16, 2, 4
NQ = NX * NC
SLOTS = 4
BLK = SLOTS * BS
ROWS = BLK + 16
CUTS = ((0, 256), (256, ROWS - 256))
SPANS = ((0, 3), (3, 2), (5, 2), (7, 2), (9, 2), (11, 2), (13, 2), (15, 1))
GROUPS = len(SPANS)
F32, BF, I32 = jnp.float32, jnp.bfloat16, jnp.int32


def dev(x, z, c, y):
    return ((x * NZ + z) * NC + c, y)


def move_kernel(
    pair_hbm, occ_hbm, int_ref, coef_ref, sums_ref,
    pair_ref, occ_ref, coef, blk, made, ct, half, relay, parts, total, tab, tabs, picked,
    loc, ring_s, ring_r, cz_s, cz_r, cy_s, cy_r, x_s, x_r, y_s, y_r, t_s, t_r, xl, yl, met,
):
    s = lax.axis_index("shell")
    y = lax.axis_index("aux")
    x, z, c = s // (NZ * NC), (s // NC) % NZ, s % NC
    q = x * NC + c
    sg = 1 - 2 * c

    loads = [
        pltpu.make_async_copy(pair_hbm, pair_ref, loc.at[0]),
        pltpu.make_async_copy(int_ref, blk.at[0, pl.ds(0, BLK)], loc.at[1]),
        pltpu.make_async_copy(occ_hbm, occ_ref, loc.at[2]),
        pltpu.make_async_copy(coef_ref, coef, loc.at[3]),
    ]
    for m in loads:
        m.start()

    barrier = pltpu.get_barrier_semaphore()
    near = [dev(x, (z + 1) % NZ, c, y), dev(x, (z + NZ - 1) % NZ, c, y), dev(x, z, 1 - c, y)]
    peers = list(near)
    peers += [dev((x + d) % NX, z, cc, y) for d in range(1, NX) for cc in range(NC)]
    peers += [dev(x, z, c, (y + d) % NY) for d in range(1, NY)]
    for p in peers:
        pl.semaphore_signal(barrier, inc=1, device_id=p, device_id_type=MESH)

    loads[0].wait()
    rid = lax.broadcasted_iota(I32, (16, BS), 0)
    k16 = (rid // 2) % SLOTS
    rv = jnp.zeros((16, BS), I32)
    for k in range(SLOTS):
        rv = jnp.where(k16 == k, pair_ref[k, 0], rv)
    rv = jnp.where(rid < 8, rv // 16, rv % 16)
    blk[0, pl.ds(BLK, 16)] = rv.astype(F32).astype(BF)
    ncol = NZ * NQ * OB
    loads[2].wait()
    lane_b = lax.broadcasted_iota(I32, (BS, ncol), 0)
    col_b = lax.broadcasted_iota(I32, (BS, ncol), 1)
    expand = jnp.where(col_b >> 3 == lane_b, 1.0, 0.0).astype(BF)
    occ8 = jnp.broadcast_to(occ_ref[...].astype(F32), (8, BS)).astype(BF)
    occ_col = jnp.dot(occ8, expand, preferred_element_type=F32)[0:1].astype(I32) * OB
    occ_col = occ_col + (lax.broadcasted_iota(I32, (1, ncol), 1) & (OB - 1))
    loads[3].wait()
    def coef_pick():
        rid = lax.broadcasted_iota(I32, (256, BS), 0)
        u, qq, o = rid >> 4, (rid >> 1) & (NQ - 1), rid & 1
        dist, other = (u + 1) >> 1, (u + 1) & 1
        zz = (z + sg * (1 - 2 * other) * dist + NZ) & (NZ - 1)
        want = (((qq >> 1) * NZ + zz) * NC + (qq & 1)) * OB + y * 2 + o
        pick = jnp.concatenate(
            [
                jnp.where(want == occ_col[:, b * BS : (b + 1) * BS], 1.0, 0.0)
                for b in range(ncol // BS)
            ],
            axis=1,
        ).astype(BF)
        got = lax.dot_general(
            pick, coef[...], (((1,), (1,)), ((), ())), preferred_element_type=F32
        )
        for k in range(SLOTS):
            local = jnp.where(pair_ref[k, 2] == 1, pair_ref[k, 1] % SLOTS, -1)
            chosen = jnp.zeros((256, BS), F32)
            for b in range(SLOTS):
                chosen += jnp.where(local == b, 1.0, 0.0) * got[:, b * BS : (b + 1) * BS]
            picked[k] = chosen.astype(BF)

    pr = lax.broadcasted_iota(I32, (256, 256), 0)
    pc = lax.broadcasted_iota(I32, (256, 256), 1)
    order = ((pr >> 1) & 3) * 64 + (pr >> 6) * 16 + ((pr >> 3) & 7) * 2 + (pr & 1)
    order = jnp.where(order == pc, 1.0, 0.0).astype(BF)

    def coef_chunk(uc):
        stack = picked[:, pl.ds(64 * uc, 64)].reshape(256, BS)
        chosen = jnp.dot(order, stack, preferred_element_type=F32).astype(BF)
        made[pl.ds(4 * uc, 4)] = chosen.reshape(4, 64, BS)
        if uc == 0:
            ct[0, y] = chosen[0:64]

    coef_pick()
    coef_chunk(0)
    coef_chunk(1)
    coef_chunk(2)
    coef_chunk(3)
    loads[1].wait()
    pl.semaphore_wait(barrier, len(peers))

    def greet(i, to):
        for p in to:
            pl.semaphore_signal(met.at[i], inc=1, device_id=p, device_id_type=MESH)

    def meet(i, n):
        pl.semaphore_wait(met.at[i], n)

    def apart(d):
        return [dev(x, (z + d) % NZ, c, y), dev(x, (z + NZ - d) % NZ, c, y)]

    pending = []

    def remote(src, dst, ss, rs, to):
        m = pltpu.make_async_remote_copy(
            src_ref=src, dst_ref=dst, send_sem=ss, recv_sem=rs, device_id=to, device_id_type=MESH
        )
        m.start()
        pending.append(m)
        return m

    def drain(keep):
        while len(pending) > keep:
            pending.pop(0).wait_send()

    nxt = dev(x, (z + sg + NZ) % NZ, c, y)
    landed = {}

    def ring(j_from, j_to, to):
        for ch, (r0, n) in enumerate(CUTS):
            if (j_from, ch) in landed:
                landed[(j_from, ch)].wait_recv()
            part = pl.ds(r0, n)
            landed[(j_to, ch)] = remote(
                blk.at[j_from, part], blk.at[j_to, part], ring_s.at[j_to, ch], ring_r.at[j_to, ch], to
            )

    def arrive(j):
        for ch in range(len(CUTS)):
            landed[(j, ch)].wait_recv()

    def step(d, e):
        j = 2 * d - 1 + e
        if d < 7 or (d == 7 and e == 0):
            ring(j, j + 2, nxt)
        else:
            arrive(j)

    ring(0, 1, nxt)
    ring(0, 16, dev(x, z, 1 - c, y))
    greet(0, near)

    cz = {}

    def coef_out(*dist):
        for d in dist:
            for e in range(2 if d < 8 else 1):
                u = 2 * d - 1 + e
                zt = (z + sg * (1 - 2 * e) * d + NZ) % NZ
                ctarget = c if e == 0 else 1 - c
                cz[u] = remote(
                    made.at[u], ct.at[u, y], cz_s.at[u], cz_r.at[u], dev(x, zt, ctarget, y)
                )

    meet(0, 3)
    greet(1, apart(2))
    ring(16, 2, nxt)
    coef_out(1)
    meet(1, 2)
    greet(2, apart(4))
    coef_out(2, 3)
    step(1, 0)
    meet(2, 2)
    step(1, 1)
    coef_out(4, 5)

    kid = (lax.broadcasted_iota(I32, (256, BS), 0) // 2) % SLOTS
    kmask = [jnp.where(kid == k, 1.0, 0.0).astype(BF) for k in range(SLOTS)]
    cy, xs, ys, xloc, yloc = {}, {}, {}, {}, {}

    def coef_aux(g):
        j0, n = SPANS[g]
        for j in range(j0, j0 + n):
            if j > 0:
                cz[j].wait_recv()
        for dy in range(1, NY):
            part = ct.at[pl.ds(j0, n), y]
            cy[(g, dy)] = remote(
                part, part, cy_s.at[g, dy], cy_r.at[g, dy], dev(x, z, c, (y + dy) % NY)
            )

    def compute(g):
        j0, n = SPANS[g]
        for dy in range(1, NY):
            cy[(g, dy)].wait_recv()
        for j in range(j0, j0 + n):
            lhs = ct[j].reshape(256, BS)
            lhs = jnp.concatenate([lhs * kmask[k] for k in range(SLOTS)], axis=1)
            h = jnp.dot(lhs, blk[j, pl.ds(0, BLK)], preferred_element_type=F32)
            h = h.reshape(NY, NQ, 8, BS)
            for qq in range(NQ):
                half[j, qq] = h[:, qq].astype(BF)
        here = pl.ds(j0, n)
        xloc[g] = pltpu.make_async_copy(half.at[here, q], relay.at[here, :, q], xl.at[g])
        xloc[g].start()
        for dq in range(1, NQ):
            qt = (q + dq) % NQ
            xs[(g, dq)] = remote(
                half.at[here, qt], relay.at[here, :, q],
                x_s.at[g, dq], x_r.at[g, dq], dev(qt // NC, z, qt % NC, y),
            )

    def to_aux(g):
        j0, n = SPANS[g]
        here = pl.ds(j0, n)
        xloc[g].wait()
        for dq in range(1, NQ):
            xs[(g, dq)].wait_recv()
        yloc[g] = pltpu.make_async_copy(relay.at[here, y], parts.at[y, here], yl.at[g])
        yloc[g].start()
        for dy in range(1, NY):
            yt = (y + dy) % NY
            ys[(g, dy)] = remote(
                relay.at[here, yt], parts.at[y, here],
                y_s.at[g, dy], y_r.at[g, dy], dev(x, z, c, yt),
            )

    def arrived(g):
        yloc[g].wait()
        for dy in range(1, NY):
            ys[(g, dy)].wait_recv()

    lane8 = lax.broadcasted_iota(I32, (8, BS), 1)
    tabled = {}

    def rows_out(i, j0, n):
        table = jnp.zeros((8, BS), F32)
        for j in range(j0, j0 + n):
            ids = blk[j, pl.ds(BLK, 16)].astype(F32)
            table = jnp.where(lane8 == j, ids[0:8] * 16.0 + ids[8:16], table)
        tab[i] = table
        tabs[i, q] = table
        for dq in range(1, NQ):
            qt = (q + dq) % NQ
            tabled[(i, dq)] = remote(
                tab.at[i], tabs.at[i, q], t_s.at[i, dq], t_r.at[i, dq], dev(qt // NC, z, qt % NC, y)
            )

    lane1 = lax.broadcasted_iota(I32, (1, BS), 1)
    code_of = {}

    def codes(i, j0, n):
        for dq in range(1, NQ):
            tabled[(i, dq)].wait_recv()
        turned = jnp.transpose(jnp.concatenate([tabs[i].reshape(64, BS)] * 2, axis=0))
        for j in range(j0, j0 + n, 2):
            both = jnp.where(lane1 < 64, turned[j : j + 1], turned[j + 1 : j + 2])
            code_of[j] = both.astype(I32) + (lane1 % 2) * 512

    def add_up(j0, n, first, last):
        code = [code_of[j] for j in range(j0, j0 + n, 2)]
        terms = jnp.concatenate(
            [parts[p, pl.ds(j0, n)].reshape(n * 64, BS) for p in range(NY)], axis=1
        )
        for t in range(4):
            row = lax.broadcasted_iota(I32, (256, BS), 0) + t * 256
            match = jnp.concatenate([jnp.where(row == v, 1.0, 0.0) for v in code], axis=1)
            got = jnp.dot(match.astype(BF), terms, preferred_element_type=F32)
            here = pl.ds(t * 256, 256)
            if first:
                total[here] = got
            elif last:
                sums_ref[here] = (total[here] + got).astype(BF)
            else:
                total[here] = total[here] + got

    coef_aux(0)
    step(2, 0)
    step(2, 1)
    coef_out(6, 7, 8)
    coef_aux(1)
    coef_aux(2)
    compute(0)
    step(3, 0)
    step(3, 1)
    coef_aux(3)
    compute(1)
    compute(2)
    to_aux(0)
    step(4, 0)
    step(4, 1)
    coef_aux(4)
    coef_aux(5)
    compute(3)
    to_aux(1)
    to_aux(2)
    drain(28)
    step(5, 0)
    step(5, 1)
    coef_aux(6)
    coef_aux(7)
    compute(4)
    to_aux(3)
    drain(28)
    step(6, 0)
    step(6, 1)
    compute(5)
    to_aux(4)
    rows_out(0, 0, 12)
    drain(34)
    step(7, 0)
    step(7, 1)
    compute(6)
    to_aux(5)
    arrived(0)
    arrived(1)
    codes(0, 0, 12)
    drain(20)
    step(8, 0)
    compute(7)
    rows_out(1, 12, 4)
    to_aux(6)
    arrived(2)
    add_up(0, 6, True, False)
    arrived(3)
    arrived(4)
    to_aux(7)
    arrived(5)
    add_up(6, 6, False, False)
    codes(1, 12, 4)
    drain(6)
    arrived(6)
    arrived(7)
    add_up(12, 4, False, True)
    drain(0)


def mix_kernel(metric_ref, sums_ref, out_ref, mixed, sems):
    ri = lax.broadcasted_iota(I32, (256, 8), 0)
    ci = lax.broadcasted_iota(I32, (256, 8), 1)
    rows4 = jnp.where(ri % 4 == ci, 1.0, 0.0)[:, 0:4].astype(BF)
    rj = lax.broadcasted_iota(I32, (8, 256), 0)
    cj = lax.broadcasted_iota(I32, (8, 256), 1)
    cols4 = jnp.where(cj // 64 == rj, 1.0, 0.0)[0:4].astype(BF)
    spread = jnp.dot(rows4, metric_ref[...], preferred_element_type=F32).astype(BF)
    spread = jnp.dot(spread, cols4, preferred_element_type=F32)
    gi = lax.broadcasted_iota(I32, (256, 256), 0)
    gj = lax.broadcasted_iota(I32, (256, 256), 1)
    mix = jnp.where(gi // 4 == gj % 64, spread, 0.0).astype(BF)
    copies = []
    for t in range(4):
        for b in range(4 * t, 4 * t + 4):
            stack = jnp.concatenate(
                [sums_ref[pl.ds(b * 64, 64), p * BS : (p + 1) * BS] for p in range(NY)], axis=0
            )
            mixed[pl.ds(b * 256, 256)] = jnp.dot(mix, stack, preferred_element_type=F32).astype(BF)
        here = pl.ds(t * 1024, 1024)
        copies.append(pltpu.make_async_copy(mixed.at[here], out_ref.at[here], sems.at[t]))
        copies[-1].start()
    for m in copies:
        m.wait()


def per_device(integrals, pair_list, coef, metric, occ_slot):
    dma = pltpu.SemaphoreType.DMA
    hbm = pl.BlockSpec(memory_space=pltpu.HBM)
    vmem = pl.BlockSpec(memory_space=pltpu.VMEM)
    operands = (pair_list, occ_slot.reshape(1, BS), integrals.reshape(BLK, BS), coef)
    sums = pl.pallas_call(
        move_kernel,
        name="move",
        out_shape=jax.ShapeDtypeStruct((1024, NY * BS), BF),
        in_specs=[hbm, hbm, hbm, hbm],
        out_specs=vmem,
        scratch_shapes=[
            pltpu.SMEM((SLOTS, 3), I32),
            pltpu.VMEM((1, BS), I32),
            pltpu.VMEM((4 * BS, 1024), BF),
            pltpu.VMEM((17, ROWS, BS), BF),
            pltpu.VMEM((NZ, 64, BS), BF),
            pltpu.VMEM((NZ, NY, 64, BS), BF),
            pltpu.VMEM((NZ, NQ, NY, 8, BS), BF),
            pltpu.VMEM((NZ, NY, NQ, 8, BS), BF),
            pltpu.VMEM((NY, NZ, NQ, 8, BS), BF),
            pltpu.VMEM((1024, NY * BS), F32),
            pltpu.VMEM((2, 8, BS), F32),
            pltpu.VMEM((2, NQ, 8, BS), F32),
            pltpu.VMEM((SLOTS, 256, BS), BF),
            dma((4,)),
            dma((17, len(CUTS))),
            dma((17, len(CUTS))),
            dma((NZ,)),
            dma((NZ,)),
            dma((GROUPS, NY)),
            dma((GROUPS, NY)),
            dma((GROUPS, NQ)),
            dma((GROUPS, NQ)),
            dma((GROUPS, NY)),
            dma((GROUPS, NY)),
            dma((2, NQ)),
            dma((2, NQ)),
            dma((GROUPS,)),
            dma((GROUPS,)),
            pltpu.SemaphoreType.REGULAR((3,)),
        ],
        compiler_params=pltpu.CompilerParams(
            collective_id=0, has_side_effects=True, vmem_limit_bytes=40 << 20
        ),
    )(*(pltpu.with_memory_space_constraint(a, pltpu.HBM) for a in operands))
    out = pl.pallas_call(
        mix_kernel,
        name="mix",
        out_shape=jax.ShapeDtypeStruct((4096, BS), BF),
        in_specs=[vmem, vmem],
        out_specs=hbm,
        scratch_shapes=[pltpu.VMEM((4096, BS), BF), dma((4,))],
        compiler_params=pltpu.CompilerParams(vmem_limit_bytes=40 << 20),
    )(metric, sums)
    return out.reshape(2, 512, NY, BS).transpose(0, 2, 1, 3).reshape(2, NY, 512 * BS)


def solution(mesh):
    placed = (P("shell", None, "aux", None), P("shell", None), P("shell", None), P(), P())
    return jax.shard_map(
        per_device,
        mesh=mesh,
        in_specs=placed,
        out_specs=P(("shell", "aux"), None, None),
        check_vma=False,
    )
```

```python
import jax
import jax.numpy as jnp
from jax import lax
from jax.experimental import pallas as pl
from jax.experimental.pallas import tpu as pltpu
from jax.sharding import PartitionSpec as P

MESH = pl.DeviceIdType.MESH
BS = 128
OB = 8
NX, NZ, NC, NY = 4, 16, 2, 4
NQ = NX * NC
SLOTS = 4
BLK = SLOTS * BS
ROWS = BLK + 16
CUTS = ((0, 256), (256, ROWS - 256))
SPANS = ((0, 3), (3, 2), (5, 2), (7, 2), (9, 2), (11, 2), (13, 2), (15, 1))
GROUPS = len(SPANS)
F32, BF, I32 = jnp.float32, jnp.bfloat16, jnp.int32


def dev(x, z, c, y):
    return ((x * NZ + z) * NC + c, y)


def move_kernel(
    pair_hbm, occ_hbm, int_ref, coef_ref, sums_ref,
    pair_ref, occ_ref, coef, blk, made, ct, half, relay, parts, total, tab, tabs, picked,
    loc, ring_s, ring_r, cz_s, cz_r, cy_s, cy_r, x_s, x_r, y_s, y_r, t_s, t_r, xl, yl, met,
):
    s = lax.axis_index("shell")
    y = lax.axis_index("aux")
    x, z, c = s // (NZ * NC), (s // NC) % NZ, s % NC
    q = x * NC + c
    sg = 1 - 2 * c

    loads = [
        pltpu.make_async_copy(pair_hbm, pair_ref, loc.at[0]),
        pltpu.make_async_copy(int_ref, blk.at[0, pl.ds(0, BLK)], loc.at[1]),
        pltpu.make_async_copy(occ_hbm, occ_ref, loc.at[2]),
        pltpu.make_async_copy(coef_ref, coef, loc.at[3]),
    ]
    for m in loads:
        m.start()

    barrier = pltpu.get_barrier_semaphore()
    near = [dev(x, (z + 1) % NZ, c, y), dev(x, (z + NZ - 1) % NZ, c, y), dev(x, z, 1 - c, y)]
    peers = list(near)
    peers += [dev((x + d) % NX, z, cc, y) for d in range(1, NX) for cc in range(NC)]
    peers += [dev(x, z, c, (y + d) % NY) for d in range(1, NY)]
    for p in peers:
        pl.semaphore_signal(barrier, inc=1, device_id=p, device_id_type=MESH)

    loads[0].wait()
    rid = lax.broadcasted_iota(I32, (16, BS), 0)
    k16 = (rid // 2) % SLOTS
    rv = jnp.zeros((16, BS), I32)
    for k in range(SLOTS):
        rv = jnp.where(k16 == k, pair_ref[k, 0], rv)
    rv = jnp.where(rid < 8, rv // 16, rv % 16)
    blk[0, pl.ds(BLK, 16)] = rv.astype(F32).astype(BF)
    ncol = NZ * NQ * OB
    loads[2].wait()
    lane_b = lax.broadcasted_iota(I32, (BS, ncol), 0)
    col_b = lax.broadcasted_iota(I32, (BS, ncol), 1)
    expand = jnp.where(col_b >> 3 == lane_b, 1.0, 0.0).astype(BF)
    occ8 = jnp.broadcast_to(occ_ref[...].astype(F32), (8, BS)).astype(BF)
    occ_col = jnp.dot(occ8, expand, preferred_element_type=F32)[0:1].astype(I32) * OB
    occ_col = occ_col + (lax.broadcasted_iota(I32, (1, ncol), 1) & (OB - 1))
    loads[3].wait()
    def coef_pick():
        rid = lax.broadcasted_iota(I32, (256, BS), 0)
        u, qq, o = rid >> 4, (rid >> 1) & (NQ - 1), rid & 1
        dist, other = (u + 1) >> 1, (u + 1) & 1
        zz = (z + sg * (1 - 2 * other) * dist + NZ) & (NZ - 1)
        want = (((qq >> 1) * NZ + zz) * NC + (qq & 1)) * OB + y * 2 + o
        pick = jnp.concatenate(
            [
                jnp.where(want == occ_col[:, b * BS : (b + 1) * BS], 1.0, 0.0)
                for b in range(ncol // BS)
            ],
            axis=1,
        ).astype(BF)
        got = lax.dot_general(
            pick, coef[...], (((1,), (1,)), ((), ())), preferred_element_type=F32
        )
        for k in range(SLOTS):
            local = jnp.where(pair_ref[k, 2] == 1, pair_ref[k, 1] % SLOTS, -1)
            chosen = jnp.zeros((256, BS), F32)
            for b in range(SLOTS):
                chosen += jnp.where(local == b, 1.0, 0.0) * got[:, b * BS : (b + 1) * BS]
            picked[k] = chosen.astype(BF)

    pr = lax.broadcasted_iota(I32, (256, 256), 0)
    pc = lax.broadcasted_iota(I32, (256, 256), 1)
    order = ((pr >> 1) & 3) * 64 + (pr >> 6) * 16 + ((pr >> 3) & 7) * 2 + (pr & 1)
    order = jnp.where(order == pc, 1.0, 0.0).astype(BF)

    def coef_chunk(uc):
        stack = picked[:, pl.ds(64 * uc, 64)].reshape(256, BS)
        chosen = jnp.dot(order, stack, preferred_element_type=F32).astype(BF)
        made[pl.ds(4 * uc, 4)] = chosen.reshape(4, 64, BS)
        if uc == 0:
            ct[0, y] = chosen[0:64]

    coef_pick()
    coef_chunk(0)
    coef_chunk(1)
    coef_chunk(2)
    coef_chunk(3)
    loads[1].wait()
    pl.semaphore_wait(barrier, len(peers))

    def greet(i, to):
        for p in to:
            pl.semaphore_signal(met.at[i], inc=1, device_id=p, device_id_type=MESH)

    def meet(i, n):
        pl.semaphore_wait(met.at[i], n)

    def apart(d):
        return [dev(x, (z + d) % NZ, c, y), dev(x, (z + NZ - d) % NZ, c, y)]

    pending = []

    def remote(src, dst, ss, rs, to):
        m = pltpu.make_async_remote_copy(
            src_ref=src, dst_ref=dst, send_sem=ss, recv_sem=rs, device_id=to, device_id_type=MESH
        )
        m.start()
        pending.append(m)
        return m

    def drain(keep):
        while len(pending) > keep:
            pending.pop(0).wait_send()

    nxt = dev(x, (z + sg + NZ) % NZ, c, y)
    landed = {}

    def ring(j_from, j_to, to):
        for ch, (r0, n) in enumerate(CUTS):
            if (j_from, ch) in landed:
                landed[(j_from, ch)].wait_recv()
            part = pl.ds(r0, n)
            landed[(j_to, ch)] = remote(
                blk.at[j_from, part], blk.at[j_to, part], ring_s.at[j_to, ch], ring_r.at[j_to, ch], to
            )

    def arrive(j):
        for ch in range(len(CUTS)):
            landed[(j, ch)].wait_recv()

    def step(d, e):
        j = 2 * d - 1 + e
        if d < 7 or (d == 7 and e == 0):
            ring(j, j + 2, nxt)
        else:
            arrive(j)

    ring(0, 1, nxt)
    ring(0, 16, dev(x, z, 1 - c, y))
    greet(0, near)

    cz = {}

    def coef_out(*dist):
        for d in dist:
            for e in range(2 if d < 8 else 1):
                u = 2 * d - 1 + e
                zt = (z + sg * (1 - 2 * e) * d + NZ) % NZ
                ctarget = c if e == 0 else 1 - c
                cz[u] = remote(
                    made.at[u], ct.at[u, y], cz_s.at[u], cz_r.at[u], dev(x, zt, ctarget, y)
                )

    meet(0, 3)
    greet(1, apart(2))
    ring(16, 2, nxt)
    coef_out(1)
    meet(1, 2)
    greet(2, apart(4))
    coef_out(2, 3)
    step(1, 0)
    meet(2, 2)
    step(1, 1)
    coef_out(4)

    kid = (lax.broadcasted_iota(I32, (256, BS), 0) // 2) % SLOTS
    kmask = [jnp.where(kid == k, 1.0, 0.0).astype(BF) for k in range(SLOTS)]
    cy, xs, ys, xloc, yloc = {}, {}, {}, {}, {}

    def coef_aux(g):
        j0, n = SPANS[g]
        for j in range(j0, j0 + n):
            if j > 0:
                cz[j].wait_recv()
        for dy in range(1, NY):
            part = ct.at[pl.ds(j0, n), y]
            cy[(g, dy)] = remote(
                part, part, cy_s.at[g, dy], cy_r.at[g, dy], dev(x, z, c, (y + dy) % NY)
            )

    def compute(g):
        j0, n = SPANS[g]
        for dy in range(1, NY):
            cy[(g, dy)].wait_recv()
        for j in range(j0, j0 + n):
            lhs = ct[j].reshape(256, BS)
            lhs = jnp.concatenate([lhs * kmask[k] for k in range(SLOTS)], axis=1)
            h = jnp.dot(lhs, blk[j, pl.ds(0, BLK)], preferred_element_type=F32)
            h = h.reshape(NY, NQ, 8, BS)
            for qq in range(NQ):
                half[j, qq] = h[:, qq].astype(BF)
        here = pl.ds(j0, n)
        xloc[g] = pltpu.make_async_copy(half.at[here, q], relay.at[here, :, q], xl.at[g])
        xloc[g].start()
        for dq in range(1, NQ):
            qt = (q + dq) % NQ
            xs[(g, dq)] = remote(
                half.at[here, qt], relay.at[here, :, q],
                x_s.at[g, dq], x_r.at[g, dq], dev(qt // NC, z, qt % NC, y),
            )

    def to_aux(g):
        j0, n = SPANS[g]
        here = pl.ds(j0, n)
        xloc[g].wait()
        for dq in range(1, NQ):
            xs[(g, dq)].wait_recv()
        yloc[g] = pltpu.make_async_copy(relay.at[here, y], parts.at[y, here], yl.at[g])
        yloc[g].start()
        for dy in range(1, NY):
            yt = (y + dy) % NY
            ys[(g, dy)] = remote(
                relay.at[here, yt], parts.at[y, here],
                y_s.at[g, dy], y_r.at[g, dy], dev(x, z, c, yt),
            )

    def arrived(g):
        yloc[g].wait()
        for dy in range(1, NY):
            ys[(g, dy)].wait_recv()

    lane8 = lax.broadcasted_iota(I32, (8, BS), 1)
    tabled = {}

    def rows_out(i, j0, n):
        table = jnp.zeros((8, BS), F32)
        for j in range(j0, j0 + n):
            ids = blk[j, pl.ds(BLK, 16)].astype(F32)
            table = jnp.where(lane8 == j, ids[0:8] * 16.0 + ids[8:16], table)
        tab[i] = table
        tabs[i, q] = table
        for dq in range(1, NQ):
            qt = (q + dq) % NQ
            tabled[(i, dq)] = remote(
                tab.at[i], tabs.at[i, q], t_s.at[i, dq], t_r.at[i, dq], dev(qt // NC, z, qt % NC, y)
            )

    lane1 = lax.broadcasted_iota(I32, (1, BS), 1)
    code_of = {}

    def codes(i, j0, n):
        for dq in range(1, NQ):
            tabled[(i, dq)].wait_recv()
        turned = jnp.transpose(jnp.concatenate([tabs[i].reshape(64, BS)] * 2, axis=0))
        for j in range(j0, j0 + n, 2):
            both = jnp.where(lane1 < 64, turned[j : j + 1], turned[j + 1 : j + 2])
            code_of[j] = both.astype(I32) + (lane1 % 2) * 512

    def add_up(j0, n, first, last):
        code = [code_of[j] for j in range(j0, j0 + n, 2)]
        terms = jnp.concatenate(
            [parts[p, pl.ds(j0, n)].reshape(n * 64, BS) for p in range(NY)], axis=1
        )
        for t in range(4):
            row = lax.broadcasted_iota(I32, (256, BS), 0) + t * 256
            match = jnp.concatenate([jnp.where(row == v, 1.0, 0.0) for v in code], axis=1)
            got = jnp.dot(match.astype(BF), terms, preferred_element_type=F32)
            here = pl.ds(t * 256, 256)
            if first:
                total[here] = got
            elif last:
                sums_ref[here] = (total[here] + got).astype(BF)
            else:
                total[here] = total[here] + got

    coef_aux(0)
    step(2, 0)
    step(2, 1)
    coef_out(5, 6)
    coef_aux(1)
    coef_aux(2)
    compute(0)
    step(3, 0)
    step(3, 1)
    coef_out(7, 8)
    coef_aux(3)
    compute(1)
    compute(2)
    to_aux(0)
    step(4, 0)
    step(4, 1)
    coef_aux(4)
    coef_aux(5)
    compute(3)
    to_aux(1)
    to_aux(2)
    drain(28)
    step(5, 0)
    step(5, 1)
    coef_aux(6)
    coef_aux(7)
    compute(4)
    to_aux(3)
    drain(28)
    step(6, 0)
    step(6, 1)
    compute(5)
    to_aux(4)
    rows_out(0, 0, 12)
    drain(34)
    step(7, 0)
    step(7, 1)
    compute(6)
    to_aux(5)
    arrived(0)
    arrived(1)
    codes(0, 0, 12)
    drain(20)
    step(8, 0)
    compute(7)
    rows_out(1, 12, 4)
    to_aux(6)
    arrived(2)
    add_up(0, 6, True, False)
    arrived(3)
    arrived(4)
    to_aux(7)
    arrived(5)
    add_up(6, 6, False, False)
    codes(1, 12, 4)
    drain(6)
    arrived(6)
    arrived(7)
    add_up(12, 4, False, True)
    drain(0)


def mix_kernel(metric_ref, sums_ref, out_ref, mixed, sems):
    ri = lax.broadcasted_iota(I32, (256, 8), 0)
    ci = lax.broadcasted_iota(I32, (256, 8), 1)
    rows4 = jnp.where(ri % 4 == ci, 1.0, 0.0)[:, 0:4].astype(BF)
    rj = lax.broadcasted_iota(I32, (8, 256), 0)
    cj = lax.broadcasted_iota(I32, (8, 256), 1)
    cols4 = jnp.where(cj // 64 == rj, 1.0, 0.0)[0:4].astype(BF)
    spread = jnp.dot(rows4, metric_ref[...], preferred_element_type=F32).astype(BF)
    spread = jnp.dot(spread, cols4, preferred_element_type=F32)
    gi = lax.broadcasted_iota(I32, (256, 256), 0)
    gj = lax.broadcasted_iota(I32, (256, 256), 1)
    mix = jnp.where(gi // 4 == gj % 64, spread, 0.0).astype(BF)
    copies = []
    for t in range(4):
        for b in range(4 * t, 4 * t + 4):
            stack = jnp.concatenate(
                [sums_ref[pl.ds(b * 64, 64), p * BS : (p + 1) * BS] for p in range(NY)], axis=0
            )
            mixed[pl.ds(b * 256, 256)] = jnp.dot(mix, stack, preferred_element_type=F32).astype(BF)
        here = pl.ds(t * 1024, 1024)
        copies.append(pltpu.make_async_copy(mixed.at[here], out_ref.at[here], sems.at[t]))
        copies[-1].start()
    for m in copies:
        m.wait()


def per_device(integrals, pair_list, coef, metric, occ_slot):
    dma = pltpu.SemaphoreType.DMA
    hbm = pl.BlockSpec(memory_space=pltpu.HBM)
    vmem = pl.BlockSpec(memory_space=pltpu.VMEM)
    operands = (pair_list, occ_slot.reshape(1, BS), integrals.reshape(BLK, BS), coef)
    sums = pl.pallas_call(
        move_kernel,
        name="move",
        out_shape=jax.ShapeDtypeStruct((1024, NY * BS), BF),
        in_specs=[hbm, hbm, hbm, hbm],
        out_specs=vmem,
        scratch_shapes=[
            pltpu.SMEM((SLOTS, 3), I32),
            pltpu.VMEM((1, BS), I32),
            pltpu.VMEM((4 * BS, 1024), BF),
            pltpu.VMEM((17, ROWS, BS), BF),
            pltpu.VMEM((NZ, 64, BS), BF),
            pltpu.VMEM((NZ, NY, 64, BS), BF),
            pltpu.VMEM((NZ, NQ, NY, 8, BS), BF),
            pltpu.VMEM((NZ, NY, NQ, 8, BS), BF),
            pltpu.VMEM((NY, NZ, NQ, 8, BS), BF),
            pltpu.VMEM((1024, NY * BS), F32),
            pltpu.VMEM((2, 8, BS), F32),
            pltpu.VMEM((2, NQ, 8, BS), F32),
            pltpu.VMEM((SLOTS, 256, BS), BF),
            dma((4,)),
            dma((17, len(CUTS))),
            dma((17, len(CUTS))),
            dma((NZ,)),
            dma((NZ,)),
            dma((GROUPS, NY)),
            dma((GROUPS, NY)),
            dma((GROUPS, NQ)),
            dma((GROUPS, NQ)),
            dma((GROUPS, NY)),
            dma((GROUPS, NY)),
            dma((2, NQ)),
            dma((2, NQ)),
            dma((GROUPS,)),
            dma((GROUPS,)),
            pltpu.SemaphoreType.REGULAR((3,)),
        ],
        compiler_params=pltpu.CompilerParams(
            collective_id=0, has_side_effects=True, vmem_limit_bytes=40 << 20
        ),
    )(*(pltpu.with_memory_space_constraint(a, pltpu.HBM) for a in operands))
    out = pl.pallas_call(
        mix_kernel,
        name="mix",
        out_shape=jax.ShapeDtypeStruct((4096, BS), BF),
        in_specs=[vmem, vmem],
        out_specs=hbm,
        scratch_shapes=[pltpu.VMEM((4096, BS), BF), dma((4,))],
        compiler_params=pltpu.CompilerParams(vmem_limit_bytes=40 << 20),
    )(metric, sums)
    return out.reshape(2, 512, NY, BS).transpose(0, 2, 1, 3).reshape(2, NY, 512 * BS)


def solution(mesh):
    placed = (P("shell", None, "aux", None), P("shell", None), P("shell", None), P(), P())
    return jax.shard_map(
        per_device,
        mesh=mesh,
        in_specs=placed,
        out_specs=P(("shell", "aux"), None, None),
        check_vma=False,
    )
```
